32 devices in a mesh: dp: 8 (over z, y), mp: 4 (over x, core).
Axes of the slice: x: 2, y: 2, z: 4, core: 2. Of those that a mesh axis runs over, the one named last changes fastest.
Arguments:
- patches: bfloat16 [24, 1024, 1280], P('dp', 'mp'), may hold values from -6 to 6
- kept_mask: int32 [24, 1024], P('dp', 'mp'), may hold values from 0 to 1, as said below
- destination: int32 [24, 1024], P('dp', 'mp'), may hold values from 0 to 7, as said below
- coefficients: bfloat16 [9, 1280, 2560], P(None, None, 'mp'), may hold values from -0.15625 to 0.15625
- cotangent: bfloat16 [6144, 2560], P('dp', 'mp'), may hold values from -3 to 3
Outputs:
- grad_patches: bfloat16 [24, 1024, 1280], P('dp', 'mp')
- grad_coefficients: float32 [9, 1280, 2560], P(None, 'dp', 'mp')
The draws below stay inside these ranges and needn't reach their ends.
Inputs may be any that keep to these rules, and one draw needn't show every extreme that they name: `kept_mask`: every image keeps the same number of patches in each of its 4 blocks, from 32 to 96; all images together keep exactly 6144 patches. For a kept patch, its balanced shard; entries of patches that are not kept are not used. Among the kept patches of one block of the 3 images of one index of dp, at most 36 have the same destination, and some index of dp has exactly 36 for every destination in every block. Every destination receives exactly 192 kept patches of each block.
All inputs are finite; a program needn't handle non-finite values.
Results may differ from the reference program's by a relative error of at most 0.0074.
Values may be sent and summed in bfloat16 or wider, within the bound.
No kernel may reach another device: no remote copies, remote signals or barrier semaphores. Data moves between devices by JAX's collectives and lax.ppermute only.
A program may use at most 192 MiB of HBM per device.

```python
import jax
import jax.numpy as jnp
from jax import lax

D = 1280
FF = 2560
NBASIS = 8
PATCHES = 1024
KEEP_IMG = 256
IMG_DEV = 3
NCH = 9
IMAGES = 24
PQ = 256
KEEP_DEV = 768
TOTAL = 6144
N_DP = 8
N_MP = 4


def permuted(row_key):
    return jax.random.permutation(row_key, PQ)


def mask_and_routes(key):
    key_swing, key_sign, key_perm, key_fill = jax.random.split(key, 4)
    base_count = KEEP_IMG // N_MP
    swing_most = KEEP_IMG // (2 * N_MP)
    pair_count = N_DP // 2
    amount = jax.random.randint(key_swing, (pair_count, IMG_DEV), 0, swing_most + 1)
    signs = jax.random.randint(key_sign, (pair_count, IMG_DEV), 0, 2) * 2 - 1
    amount = amount.at[0].set(swing_most)
    signs = signs.at[0].set(1)
    upper = base_count + signs * amount
    lower = base_count - signs * amount
    per_block = jnp.stack([upper, lower], axis=1).reshape(IMAGES)
    row_keys = jax.random.split(key_perm, IMAGES * N_MP)
    orders = jax.vmap(permuted)(row_keys).reshape(IMAGES, N_MP, PQ)
    kept = (orders < per_block[:, None, None]).astype(jnp.int32)
    in_order = kept.transpose(1, 0, 2).reshape(-1)
    rank_all = jnp.cumsum(in_order) - in_order
    filler = jax.random.randint(key_fill, in_order.shape, 0, N_DP)
    routes = jnp.where(in_order == 1, rank_all % N_DP, filler)
    routes = routes.reshape(N_MP, IMAGES, PQ).transpose(1, 0, 2).reshape(IMAGES, PATCHES)
    return (kept.reshape(IMAGES, PATCHES).astype(jnp.int32), routes.astype(jnp.int32))


def draw_kept_mask(key, part):
    return mask_and_routes(jax.random.fold_in(key, 11))[0]


def draw_destination(key, part):
    return mask_and_routes(jax.random.fold_in(key, 11))[1]


def block_levels(stream_key, extent, cuts, low, top_value):
    gain, own = 1.0, jax.random.fold_in(stream_key, 6)
    for position, shards_of in cuts:
        draws = jnp.exp(jax.random.uniform(jax.random.fold_in(own, position), (shards_of,), jnp.float32, low / len(cuts), top_value / len(cuts)))
        gain = gain * jnp.repeat(draws, extent[position] // shards_of).reshape([-1 if axis == position else 1 for axis in range(len(extent))])
    return gain


def bell_draw(rng, shape, scale, reach, cuts=(), kind=jnp.bfloat16):
    gain = block_levels(rng, shape, cuts, -0.22, 0.18) if cuts else 1.0
    values = jax.random.normal(rng, shape, jnp.float32) * scale * gain
    return jnp.minimum(jnp.maximum(values, -reach), reach).astype(kind)


def setup_inputs(seed: int = 0) -> dict:
    key_of = jax.random.split(jax.random.key(seed), 6)
    return {
        "patches": bell_draw(key_of[0], (IMAGES, PATCHES, D), 1.0, 6.0, ((0, 8), (1, 4))),
        "kept_mask": draw_kept_mask(jax.random.fold_in(key_of[5], 71), 0),
        "destination": draw_destination(jax.random.fold_in(key_of[5], 71), 0),
        "coefficients": bell_draw(key_of[3], (NCH, D, FF), D ** -0.5, 0.15625, ((2, 4),)),
        "cotangent": bell_draw(key_of[4], (TOTAL, FF), 0.2, 3.0, ((0, 8), (1, 4))),
    }


STEP_WIDTH = 0.8
FIRST_KNOT = -4.4
EPSILON = 1e-05

def inner_piece(value):
    return (((-3.0 * value + 12.0) * value - 12.0) * value + 4.0) / 6.0

def inner_slope(value):
    return ((-3.0 * value + 8.0) * value - 4.0) / 2.0

def cardinal(scaled):
    mirror = 4.0 - scaled
    result = jnp.where(scaled < 1.0, scaled * scaled * scaled / 6.0, jnp.where(scaled < 2.0, inner_piece(scaled), jnp.where(scaled < 3.0, inner_piece(mirror), mirror * mirror * mirror / 6.0)))
    return jnp.where((scaled >= 0.0) & (scaled < 4.0), result, 0.0)

def cardinal_slope(scaled):
    mirror = 4.0 - scaled
    result = jnp.where(scaled < 1.0, scaled * scaled / 2.0, jnp.where(scaled < 2.0, inner_slope(scaled), jnp.where(scaled < 3.0, -inner_slope(mirror), -mirror * mirror / 2.0)))
    return jnp.where((scaled >= 0.0) & (scaled < 4.0), result, 0.0)

def knot_offsets(values):
    knots = (FIRST_KNOT + STEP_WIDTH * jnp.arange(NBASIS).astype(jnp.float32)).reshape(1, NBASIS, 1)
    return (values[:, None, :] - knots) / STEP_WIDTH

def expand(values):
    sigmoid = jax.nn.sigmoid(values)
    return jnp.concatenate([(values * sigmoid)[:, None, :], cardinal(knot_offsets(values))], axis=1)

def expand_slope(values):
    sigmoid = jax.nn.sigmoid(values)
    base_slope = sigmoid * (1.0 + values * (1.0 - sigmoid))
    return jnp.concatenate([base_slope[:, None, :], cardinal_slope(knot_offsets(values)) / STEP_WIDTH], axis=1)

def normalize(rows):
    wide = rows.astype(jnp.float32)
    centre = lax.optimization_barrier(jnp.mean(wide, axis=1, keepdims=True))
    spread = lax.optimization_barrier(jnp.mean((wide - centre) * (wide - centre), axis=1, keepdims=True))
    inv_scale = lax.rsqrt(spread + EPSILON)
    return ((wide - centre) * inv_scale, inv_scale)

def reference(patches, kept_mask, destination, coefficients, cotangent):
    kept_order = kept_mask.reshape(IMAGES, N_MP, PQ).transpose(1, 0, 2).reshape(-1)
    dest_order = destination.reshape(IMAGES, N_MP, PQ).transpose(1, 0, 2).reshape(-1)
    is_kept = kept_order == 1
    shards = jnp.arange(N_DP).astype(jnp.int32)
    onehot = ((dest_order[:, None] == shards[None, :]) & is_kept[:, None]).astype(jnp.int32)
    earlier = jnp.cumsum(onehot, axis=0).astype(jnp.int32) - onehot
    rank_same = lax.optimization_barrier(jnp.sum(earlier * onehot, axis=1)).astype(jnp.int32)
    row_index = jnp.where(is_kept, dest_order * KEEP_DEV + rank_same, TOTAL).astype(jnp.int32)
    rows_order = patches.reshape(IMAGES, N_MP, PQ, D).transpose(1, 0, 2, 3).reshape(IMAGES * PATCHES, D)
    balanced = jnp.zeros((TOTAL, D), jnp.bfloat16).at[row_index].set(rows_order, mode='drop')
    coef_table = coefficients.reshape(NCH * D, FF)
    row_blocks = balanced.reshape(N_DP, KEEP_DEV, D)
    cot_blocks = cotangent.reshape(N_DP, KEEP_DEV, FF)

    def one_block(running, pair):
        block_rows, cot_rows = pair
        centred, inv_scale = normalize(block_rows)
        normed = centred.astype(jnp.bfloat16)
        normed_wide = normed.astype(jnp.float32)
        expanded = expand(normed_wide).astype(jnp.bfloat16).reshape(KEEP_DEV, NCH * D)
        running = running + jnp.dot(expanded.T, cot_rows, preferred_element_type=jnp.float32)
        hidden_grad = jnp.dot(cot_rows, coef_table.T, preferred_element_type=jnp.float32).reshape(KEEP_DEV, NCH, D)
        normed_grad = lax.optimization_barrier(jnp.sum(hidden_grad * expand_slope(normed_wide), axis=1))
        first_mean = lax.optimization_barrier(jnp.mean(normed_grad, axis=1, keepdims=True))
        second_mean = lax.optimization_barrier(jnp.mean(normed_grad * centred, axis=1, keepdims=True))
        row_grad = inv_scale * (normed_grad - first_mean - centred * second_mean)
        return (running, row_grad.astype(jnp.bfloat16))
    grad_table, grads = lax.scan(one_block, jnp.zeros((NCH * D, FF), jnp.float32), (row_blocks, cot_blocks))
    grads = grads.reshape(TOTAL, D)
    clamped = jnp.minimum(row_index, TOTAL - 1)
    back_rows = jnp.where(is_kept[:, None], grads[clamped], jnp.zeros((), jnp.bfloat16))
    grad_patches = back_rows.reshape(N_MP, IMAGES, PQ, D).transpose(1, 0, 2, 3).reshape(IMAGES, PATCHES, D)
    return (grad_patches, grad_table.reshape(NCH, D, FF))
```

```python
import functools

import jax
import jax.numpy as jnp
import numpy as np
from jax import lax
from jax.experimental import pallas as pl
from jax.experimental.pallas import tpu as pltpu
from jax.sharding import PartitionSpec as P

KEEP_IMG = 256
FIRST_KNOT = -4.4
INV_STEP = 1.25
EPSILON = 1e-05
BF = jnp.bfloat16
F32 = jnp.float32
NBASIS = 8
PARAMS = pltpu.CompilerParams(vmem_limit_bytes=58 * 2**20)


def cost(flops, moved):
    return pl.CostEstimate(flops=int(flops), transcendentals=0, bytes_accessed=int(moved))


def cell_of(wide):
    scaled = (wide - FIRST_KNOT) * INV_STEP
    cell = jnp.floor(scaled)
    frac = scaled - cell
    legal = (cell >= 0.0) & (cell <= 10.0)
    return jnp.where(legal, cell, 11.0), frac


def bits_of(cell):
    low = cell
    bits = []
    for weight in (8.0, 4.0, 2.0):
        has = low >= weight
        low = jnp.where(has, low - weight, low)
        bits.append(has)
    bits.append(low >= 1.0)
    return bits


def sigmoid(wide):
    return 1.0 / (1.0 + jnp.exp(-wide))


def spread_basis(wide):
    cell, frac = cell_of(wide)
    bit8, bit4, bit2, bit1 = bits_of(cell.astype(BF))
    square = frac * frac
    cube = square * frac
    mirror = 1.0 - frac
    p0 = cube * (1.0 / 6.0)
    p1 = (1.0 + 3.0 * (frac + square - cube)) * (1.0 / 6.0)
    p2 = (4.0 - 6.0 * square + 3.0 * cube) * (1.0 / 6.0)
    p3 = mirror * mirror * mirror * (1.0 / 6.0)
    lane = [p.astype(BF) for p in (p3, p2, p1, p0)]
    zero = jnp.zeros_like(lane[0])

    def at(items, index):
        return items[index] if 0 <= index < len(items) else zero

    for bit, shift, size in ((bit1, 1, 5), (bit2, 2, 7), (bit4, 4, 11)):
        lane = [jnp.where(bit, at(lane, i - shift), at(lane, i)) for i in range(size)]
    tops = [jnp.where(bit8, at(lane, i - 8), at(lane, i)) for i in range(3, 11)]
    return [(wide * sigmoid(wide)).astype(BF)] + tops


def slope_sum(wide, base_grad, grads):
    cell, frac = cell_of(wide)
    bit8, bit4, bit2, bit1 = bits_of(cell.astype(BF))
    zero = jnp.zeros_like(grads[0])
    row = [zero] * 3 + grads + [zero] * 4
    row = [jnp.where(bit8, row[i + 8], row[i]) if i < 7 else row[i] for i in range(11)]
    row = [jnp.where(bit4, row[i + 4], row[i]) for i in range(7)]
    row = [jnp.where(bit2, row[i + 2], row[i]) for i in range(5)]
    row = [jnp.where(bit1, row[i + 1], row[i]) for i in range(4)]
    half = 0.5 * INV_STEP
    square3 = 3.0 * frac * frac
    mirror = 1.0 - frac
    q0 = frac * frac
    q1 = 1.0 + 2.0 * frac - square3
    q2 = square3 - 4.0 * frac
    q3 = -(mirror * mirror)
    spline = q0 * row[3].astype(F32) + q1 * row[2].astype(F32)
    spline = spline + q2 * row[1].astype(F32) + q3 * row[0].astype(F32)
    sig = sigmoid(wide)
    return spline * half + base_grad.astype(F32) * (sig * (1.0 + wide * (1.0 - sig)))


def send_kernel(n_dest, slots, capacity, kept_ref, dest_ref, rows_ref, out_ref, at_ref):
    images = kept_ref.shape[0]
    total = n_dest * slots
    kept = jnp.concatenate([kept_ref[i : i + 1, :] for i in range(images)], axis=1)
    dest = jnp.concatenate([dest_ref[i : i + 1, :] for i in range(images)], axis=1)
    count = kept.shape[1]
    padded = max(16, n_dest)
    shard = lax.broadcasted_iota(jnp.int32, (padded, count), 0)
    onehot = jnp.where((shard == dest) & (kept == 1), 1.0, 0.0).astype(F32)
    before = (
        lax.broadcasted_iota(jnp.int32, (count, count), 0)
        < lax.broadcasted_iota(jnp.int32, (count, count), 1)
    ).astype(F32).astype(BF)
    earlier = jnp.dot(onehot.astype(BF), before, preferred_element_type=F32)
    rank = jnp.sum((earlier + shard.astype(F32) * slots) * onehot, axis=0, keepdims=True)
    place = jnp.where(kept == 1, rank, -1.0).astype(jnp.int32)
    at_ref[...] = place
    pick = (lax.broadcasted_iota(jnp.int32, (total, count), 0) == place).astype(F32).astype(BF)
    moved = jnp.dot(pick, rows_ref[...], preferred_element_type=F32)
    counts = jnp.sum(onehot, axis=1, keepdims=True)
    counts = jnp.broadcast_to(counts, (padded, rows_ref.shape[1])).astype(BF)
    marks = (
        lax.broadcasted_iota(jnp.int32, (total, padded), 0)
        == lax.broadcasted_iota(jnp.int32, (total, padded), 1) * slots + capacity
    ).astype(F32).astype(BF)
    out_ref[...] = (moved + jnp.dot(marks, counts, preferred_element_type=F32)).astype(BF)


def arrive_kernel(
    n_dest, slots, capacity, own, in_ref, norm_ref, feat_ref, wide_ref, inv_ref, pick_ref, hold
):
    width = -(-own // 128) * 128
    row = lax.broadcasted_iota(jnp.int32, (slots, width), 0).astype(F32)
    lane = lax.broadcasted_iota(jnp.int32, (slots, width), 1).astype(F32)
    base = (capacity // 8) * 8
    start = jnp.zeros((1, width), F32)
    for source in range(n_dest):
        tile = in_ref[source, base : base + 8, 0:width].astype(F32)
        held = tile[capacity - base : capacity - base + 1, :]
        hit = (row < held) & (lane == start + row)
        hold[source * slots : (source + 1) * slots, :] = jnp.where(hit, 1.0, 0.0)
        start = start + held
    pick = hold[...].astype(BF)
    pick_ref[...] = pick
    rows = in_ref[...].reshape(n_dest * slots, in_ref.shape[2])
    local = lax.dot_general(pick, rows, (((0,), (0,)), ((), ())), preferred_element_type=F32)
    centre = jnp.mean(local, axis=1, keepdims=True)
    centred = local - centre
    spread = jnp.mean(centred * centred, axis=1, keepdims=True)
    inv = lax.rsqrt(spread + EPSILON)
    centred = centred * inv
    wide_ref[...] = centred[0:own]
    inv_ref[...] = jnp.broadcast_to(inv, (width, 128))[0:own]
    normed = centred[0:own].astype(BF)
    norm_ref[...] = normed
    turned = jnp.transpose(centred)
    step = turned.shape[0] // n_dest
    for dest in range(n_dest):
        upper = turned[dest * step : dest * step + step // 2, 0:own]
        lower = turned[dest * step + step // 2 : (dest + 1) * step, 0:own]
        feat_ref[dest] = jnp.concatenate([upper, lower], axis=1).astype(BF)


def hidden_kernel(cot_ref, coef_ref, out_ref):
    features = coef_ref.shape[1]
    for first in range(0, features, 256):
        out_ref[0, :, first : first + 256] = lax.dot_general(
            cot_ref[...],
            coef_ref[0, first : first + 256, :],
            (((1,), (1,)), ((), ())),
            preferred_element_type=F32,
        ).astype(BF)


def slope_kernel(groups, meta_ref, *refs):
    grads, value_ref, out_ref = refs[:groups], refs[groups], refs[groups + 1]
    rows, width = value_ref.shape

    def step(index, carry):
        span = pl.ds(pl.multiple_of(index * 16, 16), 16)
        wide = value_ref[span, :].astype(F32)
        parts = []
        for ref in grads:
            parts += [ref[c, span, :] for c in range(ref.shape[0])]
        out_ref[span, :] = slope_sum(wide, parts[0], parts[1:]).astype(out_ref.dtype)
        return carry

    lax.fori_loop(0, rows // 16, step, 0)


def merge_kernel(meta_ref, own_ref, core_ref, far_ref, diag_ref, out_ref):
    here = meta_ref[0]
    own, core, far, diag = own_ref[0], core_ref[0], far_ref[0], diag_ref[0]
    odd, high = lax.rem(here, 2) == 1, here >= 2

    def order(flag, first, second):
        return jnp.where(flag, second, first), jnp.where(flag, first, second)

    near = order(odd, own.astype(F32), core.astype(F32))
    away = order(odd, far.astype(F32), diag.astype(F32))
    low0, high0 = order(high, near[0], away[0])
    low1, high1 = order(high, near[1], away[1])
    pieces = [low0, low1, high0, high1]
    half = own.shape[0]
    count = own.shape[1] // 2
    upper = jnp.concatenate([piece[:, 0:count] for piece in pieces], axis=1)
    lower = jnp.concatenate([piece[:, count:] for piece in pieces], axis=1)
    out_ref[0, 0:half, :] = upper.astype(BF)
    out_ref[0, half:, :] = lower.astype(BF)


def table_kernel(spans, has_start, meta_ref, *refs):
    count = len(spans)
    values, cots = refs[:count], refs[count : 2 * count]
    start_ref = refs[2 * count] if has_start else None
    out_ref, hold = refs[-2], refs[-1]
    features = values[0].shape[1]
    hidden = cots[0].shape[1]
    for index, (low, high) in enumerate(spans):
        value_ref = values[index]

        def fill(span, value_ref=value_ref, low=low, high=high):
            for first in range(low, high, 128):
                wide = value_ref[0, span, first : first + 128].astype(F32)
                for channel, item in enumerate(spread_basis(wide)):
                    hold[channel, span, first - low : first - low + 128] = item

        def step(block, carry, fill=fill):
            fill(pl.ds(pl.multiple_of(block * 16, 16), 16))
            return carry

        if features % 16 == 0:
            lax.fori_loop(0, features // 16, step, 0)
        else:
            fill(slice(0, features))
        for channel in range(out_ref.shape[0]):
            total = jnp.dot(
                hold[channel, :, 0 : high - low], cots[index][...], preferred_element_type=F32
            )
            if index == 0 and has_start:
                total = total + start_ref[channel]
            if index > 0:
                total = total + out_ref[channel]
            out_ref[channel] = total


def reduce_kernel(own_ref, core_ref, far_ref, wide_ref, inv_ref, pick_ref, out_ref):
    grad = own_ref[...] + core_ref[...].astype(F32) + far_ref[...].astype(F32)
    wide = wide_ref[...]
    first = jnp.mean(grad, axis=1, keepdims=True)
    second = jnp.mean(grad * wide, axis=1, keepdims=True)
    row_grad = (inv_ref[:, 0:1] * (grad - first - wide * second)).astype(BF)
    own = row_grad.shape[0]
    back = jnp.dot(pick_ref[:, 0:own], row_grad, preferred_element_type=F32)
    out_ref[...] = back.astype(BF).reshape(out_ref.shape)


def place_kernel(at_ref, back_ref, out_ref):
    total = back_ref.shape[0] * back_ref.shape[1]
    count = at_ref.shape[1]
    pick = (lax.broadcasted_iota(jnp.int32, (total, count), 0) == at_ref[...]).astype(F32)
    back = back_ref[...].reshape(total, back_ref.shape[2])
    out_ref[...] = lax.dot_general(
        pick.astype(BF), back, (((0,), (0,)), ((), ())), preferred_element_type=F32
    ).astype(BF)


def ring_of(n_dp):
    if n_dp == 8:
        return [0, 2, 4, 6, 7, 5, 3, 1]
    order = []
    for block in range(n_dp // 4):
        line = list(range(block * 4, block * 4 + 4))
        order += line if block % 2 == 0 else line[::-1]
    return order


def on_device(patches, kept_mask, destination, coefficients, cotangent):
    n_dp = lax.axis_size("dp")
    n_mp = lax.axis_size("mp")
    img_dev, block_len, features = patches.shape
    channels, _, hidden = coefficients.shape
    capacity = img_dev * (KEEP_IMG // n_mp + KEEP_IMG // (2 * n_mp)) // n_dp
    slots = -(-(capacity + 1) // 8) * 8
    own = img_dev * (KEEP_IMG // n_mp)
    all_rows = own * n_mp
    patch_count = img_dev * block_len
    share = features // n_dp
    width = -(-own // 128) * 128

    ring = ring_of(n_dp)
    n_steps = n_dp // 2
    place = {device: index for index, device in enumerate(ring)}
    table = np.zeros((n_dp, n_mp, 4 + n_dp), np.int32)
    for device in range(n_dp):
        for part in range(n_mp):
            for k in range(4):
                table[device, part, k] = part ^ k
            for shift in range(n_dp):
                table[device, part, 4 + shift] = ring[(place[device] - shift) % n_dp]
    index = lax.axis_index("dp") * n_mp + lax.axis_index("mp")
    meta = lax.dynamic_index_in_dim(
        jnp.asarray(table.reshape(n_dp * n_mp, -1)), index, 0, keepdims=False
    )
    forth = [(ring[i], ring[(i + 1) % n_dp]) for i in range(n_dp)]
    back = [(b, a) for a, b in forth]
    swap_core = [(i, i ^ 1) for i in range(n_mp)]
    swap_far = [(i, i ^ 2) for i in range(n_mp)]

    def vm(shape, dtype):
        return jax.ShapeDtypeStruct(shape, dtype)

    outgoing, at = pl.pallas_call(
        functools.partial(send_kernel, n_dp, slots, capacity),
        out_shape=(vm((n_dp * slots, features), BF), vm((1, patch_count), jnp.int32)),
        compiler_params=PARAMS,
        cost_estimate=cost(2 * n_dp * slots * patch_count * features, 4 * 2**20),
        name="send",
    )(kept_mask, destination, patches.reshape(patch_count, features))
    arrived = lax.all_to_all(
        outgoing.reshape(n_dp, slots, features), "dp", split_axis=0, concat_axis=0
    )

    rounds = []
    right = left = cotangent
    for _ in range(n_steps - 1):
        right = lax.ppermute(right, "dp", forth)
        left = lax.ppermute(left, "dp", back)
        rounds.append((right, left))
    half = all_rows // 2
    rounds.append(
        (lax.ppermute(right[:half], "dp", forth), lax.ppermute(left[half:], "dp", back))
    )

    group = 3
    hidden_grads = []
    for first in range(0, channels, group):
        hidden_grads.append(
            pl.pallas_call(
                hidden_kernel,
                grid=(group,),
                in_specs=[
                    pl.BlockSpec((all_rows, hidden), lambda c: (0, 0)),
                    pl.BlockSpec((1, features, hidden), lambda c, first=first: (c + first, 0, 0)),
                ],
                out_specs=pl.BlockSpec((1, all_rows, features), lambda c: (c, 0, 0)),
                out_shape=vm((group, all_rows, features), BF),
                compiler_params=PARAMS,
                cost_estimate=cost(
                    2 * group * all_rows * features * hidden,
                    group * features * (hidden + all_rows) * 2,
                ),
                name="hidden",
            )(cotangent, coefficients)
        )

    normed, feats, centred, inv_scale, pick = pl.pallas_call(
        functools.partial(arrive_kernel, n_dp, slots, capacity, own),
        out_shape=(
            vm((own, features), BF),
            vm((n_dp, share // 2, 2 * own), BF),
            vm((own, features), F32),
            vm((own, 128), F32),
            vm((n_dp * slots, width), BF),
        ),
        scratch_shapes=[pltpu.VMEM((n_dp * slots, width), F32)],
        compiler_params=PARAMS,
        cost_estimate=cost(2 * n_dp * slots * width * features, 4 * 2**20),
        name="arrive",
    )(arrived)

    norm_core = lax.ppermute(normed, "mp", swap_core)
    norm_far = lax.ppermute(normed, "mp", swap_far)
    norm_diag = lax.ppermute(norm_far, "mp", swap_core)

    def slope(values, k, dtype):
        block = 256
        return pl.pallas_call(
            functools.partial(slope_kernel, len(hidden_grads)),
            grid_spec=pltpu.PrefetchScalarGridSpec(
                num_scalar_prefetch=1,
                grid=(features // block,),
                in_specs=[
                    pl.BlockSpec((group, own, block), lambda f, meta, k=k: (0, meta[k], f))
                    for _ in hidden_grads
                ]
                + [pl.BlockSpec((own, block), lambda f, meta: (0, f))],
                out_specs=pl.BlockSpec((own, block), lambda f, meta: (0, f)),
            ),
            out_shape=vm((own, features), dtype),
            compiler_params=PARAMS,
            cost_estimate=cost(4e9, channels * own * features * 2),
            name="slope",
        )(meta, *hidden_grads, values)

    part_core = slope(norm_core, 1, BF)
    part_own = slope(normed, 0, F32)
    part_diag = slope(norm_diag, 3, BF)
    part_far = slope(norm_far, 2, F32)
    got_own = lax.ppermute(part_core, "mp", swap_core)
    got_far = lax.ppermute(part_diag, "mp", swap_core)
    far_sum = (part_far + got_far.astype(F32)).astype(BF)
    got_sum = lax.ppermute(far_sum, "mp", swap_far)

    back_slots = pl.pallas_call(
        reduce_kernel,
        out_shape=vm((n_dp, slots, features), BF),
        compiler_params=PARAMS,
        cost_estimate=cost(2 * n_dp * slots * own * features, 4 * 2**20),
        name="reduce",
    )(part_own, got_own, got_sum, centred, inv_scale, pick)
    returned = lax.all_to_all(back_slots, "dp", split_axis=0, concat_axis=0)
    owner_rows = pl.pallas_call(
        place_kernel,
        out_shape=vm((patch_count, features), BF),
        compiler_params=PARAMS,
        cost_estimate=cost(2 * n_dp * slots * patch_count * features, 3 * 2**20),
        name="place",
    )(at, returned)

    feat_own = lax.all_to_all(feats, "dp", split_axis=0, concat_axis=0)
    feat_core = lax.ppermute(feat_own, "mp", swap_core)
    feat_far = lax.ppermute(feat_own, "mp", swap_far)
    feat_diag = lax.ppermute(feat_far, "mp", swap_core)
    merge_spec = pl.BlockSpec((1, share // 2, 2 * own), lambda s, meta: (s, 0, 0))
    values = pl.pallas_call(
        merge_kernel,
        grid_spec=pltpu.PrefetchScalarGridSpec(
            num_scalar_prefetch=1,
            grid=(n_dp,),
            in_specs=[merge_spec] * 4,
            out_specs=pl.BlockSpec((1, share, all_rows), lambda s, meta: (s, 0, 0)),
        ),
        out_shape=vm((n_dp, share, all_rows), BF),
        compiler_params=PARAMS,
        cost_estimate=cost(1e9, 4 * 2**20),
        name="merge",
    )(meta, feat_own, feat_core, feat_far, feat_diag)

    def table_sum(items, running):
        spans = [span for _, _, span in items]
        value_specs = [
            pl.BlockSpec((1, share, all_rows), lambda i, meta, shift=shift: (meta[4 + shift], 0, 0))
            for shift, _, _ in items
        ]
        cot_specs = [pl.BlockSpec(cot.shape, lambda i, meta: (0, 0)) for _, cot, _ in items]
        whole = pl.BlockSpec((channels, share, hidden), lambda i, meta: (0, 0, 0))
        extra = [] if running is None else [running]
        rows = sum(high - low for low, high in spans)
        return pl.pallas_call(
            functools.partial(table_kernel, spans, bool(extra)),
            grid_spec=pltpu.PrefetchScalarGridSpec(
                num_scalar_prefetch=1,
                grid=(1,),
                in_specs=value_specs + cot_specs + [whole] * len(extra),
                out_specs=whole,
                scratch_shapes=[pltpu.VMEM((channels, share, all_rows), BF)],
            ),
            out_shape=vm((channels, share, hidden), F32),
            compiler_params=PARAMS,
            cost_estimate=cost(4 * channels * share * hidden * rows, 8 * 2**20),
            name="table",
        )(meta, *([values] * len(items)), *[cot for _, cot, _ in items], *extra)

    running = None
    items = [(0, cotangent, (0, all_rows))]
    for step, (right, left) in enumerate(rounds, 1):
        if step < n_steps:
            items += [(step, right, (0, all_rows)), (n_dp - step, left, (0, all_rows))]
        else:
            items += [(step, right, (0, half)), (step, left, (half, all_rows))]
        running = table_sum(items, running)
        items = []

    return (owner_rows.reshape(img_dev, block_len, features), running)


def solution(mesh):
    in_specs = (
        P("dp", "mp", None),
        P("dp", "mp"),
        P("dp", "mp"),
        P(None, None, "mp"),
        P("dp", "mp"),
    )
    out_specs = (P("dp", "mp", None), P(None, "dp", "mp"))
    return jax.shard_map(
        on_device, mesh=mesh, in_specs=in_specs, out_specs=out_specs, check_vma=False
    )
```

```python
import functools

import jax
import jax.numpy as jnp
import numpy as np
from jax import lax
from jax.experimental import pallas as pl
from jax.experimental.pallas import tpu as pltpu
from jax.sharding import PartitionSpec as P

KEEP_IMG = 256
FIRST_KNOT = -4.4
INV_STEP = 1.25
EPSILON = 1e-05
BF = jnp.bfloat16
F32 = jnp.float32
NBASIS = 8
PARAMS = pltpu.CompilerParams(vmem_limit_bytes=58 * 2**20)


def cost(flops, moved):
    return pl.CostEstimate(flops=int(flops), transcendentals=0, bytes_accessed=int(moved))


def cell_of(wide):
    scaled = (wide - FIRST_KNOT) * INV_STEP
    cell = jnp.floor(scaled)
    frac = scaled - cell
    legal = (cell >= 0.0) & (cell <= 10.0)
    return jnp.where(legal, cell, 11.0), frac


def bits_of(cell):
    low = cell
    bits = []
    for weight in (8.0, 4.0, 2.0):
        has = low >= weight
        low = jnp.where(has, low - weight, low)
        bits.append(has)
    bits.append(low >= 1.0)
    return bits


def sigmoid(wide):
    return 0.5 * jnp.tanh(0.5 * wide) + 0.5


def spread_basis(wide):
    cell, frac = cell_of(wide)
    bit8, bit4, bit2, bit1 = bits_of(cell.astype(BF))
    square = frac * frac
    cube = square * frac
    mirror = 1.0 - frac
    p0 = cube * (1.0 / 6.0)
    p1 = (1.0 + 3.0 * (frac + square - cube)) * (1.0 / 6.0)
    p2 = (4.0 - 6.0 * square + 3.0 * cube) * (1.0 / 6.0)
    p3 = mirror * mirror * mirror * (1.0 / 6.0)
    lane = [p.astype(BF) for p in (p3, p2, p1, p0)]
    zero = jnp.zeros_like(lane[0])

    def at(items, index):
        return items[index] if 0 <= index < len(items) else zero

    for bit, shift, size in ((bit1, 1, 5), (bit2, 2, 7), (bit4, 4, 11)):
        lane = [jnp.where(bit, at(lane, i - shift), at(lane, i)) for i in range(size)]
    tops = [jnp.where(bit8, at(lane, i - 8), at(lane, i)) for i in range(3, 11)]
    return [(wide * sigmoid(wide)).astype(BF)] + tops


def slope_sum(wide, base_grad, grads):
    cell, frac = cell_of(wide)
    bit8, bit4, bit2, bit1 = bits_of(cell.astype(BF))
    zero = jnp.zeros_like(grads[0])
    row = [zero] * 3 + grads + [zero] * 4
    row = [jnp.where(bit8, row[i + 8], row[i]) if i < 7 else row[i] for i in range(11)]
    row = [jnp.where(bit4, row[i + 4], row[i]) for i in range(7)]
    row = [jnp.where(bit2, row[i + 2], row[i]) for i in range(5)]
    row = [jnp.where(bit1, row[i + 1], row[i]) for i in range(4)]
    half = 0.5 * INV_STEP
    square3 = 3.0 * frac * frac
    mirror = 1.0 - frac
    q0 = frac * frac
    q1 = 1.0 + 2.0 * frac - square3
    q2 = square3 - 4.0 * frac
    q3 = -(mirror * mirror)
    spline = q0 * row[3].astype(F32) + q1 * row[2].astype(F32)
    spline = spline + q2 * row[1].astype(F32) + q3 * row[0].astype(F32)
    sig = sigmoid(wide)
    return spline * half + base_grad.astype(F32) * (sig * (1.0 + wide * (1.0 - sig)))


def send_kernel(n_dest, slots, capacity, kept_ref, dest_ref, rows_ref, out_ref, at_ref):
    images = kept_ref.shape[0]
    total = n_dest * slots
    kept = jnp.concatenate([kept_ref[i : i + 1, :] for i in range(images)], axis=1)
    dest = jnp.concatenate([dest_ref[i : i + 1, :] for i in range(images)], axis=1)
    count = kept.shape[1]
    padded = max(16, n_dest)
    shard = lax.broadcasted_iota(jnp.int32, (padded, count), 0)
    onehot = jnp.where((shard == dest) & (kept == 1), 1.0, 0.0).astype(F32)
    before = (
        lax.broadcasted_iota(jnp.int32, (count, count), 0)
        < lax.broadcasted_iota(jnp.int32, (count, count), 1)
    ).astype(F32).astype(BF)
    earlier = jnp.dot(onehot.astype(BF), before, preferred_element_type=F32)
    rank = jnp.sum((earlier + shard.astype(F32) * slots) * onehot, axis=0, keepdims=True)
    place = jnp.where(kept == 1, rank, -1.0).astype(jnp.int32)
    at_ref[...] = place
    pick = (lax.broadcasted_iota(jnp.int32, (total, count), 0) == place).astype(F32).astype(BF)
    moved = jnp.dot(pick, rows_ref[...], preferred_element_type=F32)
    counts = jnp.sum(onehot, axis=1, keepdims=True)
    counts = jnp.broadcast_to(counts, (padded, rows_ref.shape[1])).astype(BF)
    marks = (
        lax.broadcasted_iota(jnp.int32, (total, padded), 0)
        == lax.broadcasted_iota(jnp.int32, (total, padded), 1) * slots + capacity
    ).astype(F32).astype(BF)
    out_ref[...] = (moved + jnp.dot(marks, counts, preferred_element_type=F32)).astype(BF)


def arrive_kernel(
    n_dest, slots, capacity, own, in_ref, norm_ref, feat_ref, wide_ref, inv_ref, pick_ref, hold
):
    width = -(-own // 128) * 128
    row = lax.broadcasted_iota(jnp.int32, (slots, width), 0).astype(F32)
    lane = lax.broadcasted_iota(jnp.int32, (slots, width), 1).astype(F32)
    base = (capacity // 8) * 8
    start = jnp.zeros((1, width), F32)
    for source in range(n_dest):
        tile = in_ref[source, base : base + 8, 0:width].astype(F32)
        held = tile[capacity - base : capacity - base + 1, :]
        hit = (row < held) & (lane == start + row)
        hold[source * slots : (source + 1) * slots, :] = jnp.where(hit, 1.0, 0.0)
        start = start + held
    pick = hold[...].astype(BF)
    pick_ref[...] = pick
    rows = in_ref[...].reshape(n_dest * slots, in_ref.shape[2])
    local = lax.dot_general(pick, rows, (((0,), (0,)), ((), ())), preferred_element_type=F32)
    centre = jnp.mean(local, axis=1, keepdims=True)
    centred = local - centre
    spread = jnp.mean(centred * centred, axis=1, keepdims=True)
    inv = lax.rsqrt(spread + EPSILON)
    centred = centred * inv
    wide_ref[...] = centred[0:own]
    inv_ref[...] = jnp.broadcast_to(inv, (width, 128))[0:own]
    normed = centred[0:own].astype(BF)
    norm_ref[...] = normed
    turned = jnp.transpose(centred)
    step = turned.shape[0] // n_dest
    for dest in range(n_dest):
        upper = turned[dest * step : dest * step + step // 2, 0:own]
        lower = turned[dest * step + step // 2 : (dest + 1) * step, 0:own]
        feat_ref[dest] = jnp.concatenate([upper, lower], axis=1).astype(BF)


def hidden_kernel(cot_ref, coef_ref, out_ref):
    features = coef_ref.shape[1]
    for first in range(0, features, 256):
        out_ref[0, :, first : first + 256] = lax.dot_general(
            cot_ref[...],
            coef_ref[0, first : first + 256, :],
            (((1,), (1,)), ((), ())),
            preferred_element_type=F32,
        ).astype(BF)


def slope_kernel(groups, meta_ref, *refs):
    grads, value_ref, out_ref = refs[:groups], refs[groups], refs[groups + 1]
    rows, width = value_ref.shape

    def step(index, carry):
        span = pl.ds(pl.multiple_of(index * 16, 16), 16)
        wide = value_ref[span, :].astype(F32)
        parts = []
        for ref in grads:
            parts += [ref[c, span, :] for c in range(ref.shape[0])]
        out_ref[span, :] = slope_sum(wide, parts[0], parts[1:]).astype(out_ref.dtype)
        return carry

    lax.fori_loop(0, rows // 16, step, 0)


def table_kernel(shifts, halves, has_start, own, chunk, meta_ref, *refs):
    values, cots = refs[:4], refs[4 : -6 if has_start else -5]
    start_ref = refs[-6] if has_start else None
    out_ref, joined, rows = refs[-5], refs[-2], refs[-1]
    holds = refs[-4:-2]
    half = values[0].shape[1]
    features = 2 * half
    channels = out_ref.shape[0]
    blocks = features // chunk

    def join(index):
        source = meta_ref[4 + shifts[index]]
        for slot in range(4):
            piece = values[slot][source].astype(F32)
            joined[0:half, slot * own : (slot + 1) * own] = piece[:, 0:own]
            joined[half:features, slot * own : (slot + 1) * own] = piece[:, own:]
        for part in range(4):
            slot = pl.ds(pl.multiple_of(meta_ref[part] * own, 16), own)
            if index == halves:
                source_ref = cots[index + part // 2]
                taken = source_ref[(part % 2) * own : (part % 2 + 1) * own, :]
            else:
                taken = cots[index][part * own : (part + 1) * own, :]
            rows[index % 2, slot, :] = taken

    def fill(index, block):
        for low in range(0, chunk, 16):
            high = min(low + 16, chunk)
            span = pl.ds(pl.multiple_of(block * chunk + low, 8), high - low)
            for first in range(0, 4 * own, 256):
                wide = joined[span, first : first + 256]
                for channel, item in enumerate(spread_basis(wide)):
                    holds[index % 2][block, channel, low:high, first : first + 256] = item

    def multiply(index, block):
        span = pl.ds(pl.multiple_of(block * chunk, 8), chunk)
        right = rows[index % 2]
        old = start_ref if index == 0 else out_ref
        if chunk % 16 == 0:
            left = holds[index % 2][block].reshape(channels * chunk, 4 * own)
            total = jnp.dot(left, right, preferred_element_type=F32)
            total = total.reshape(channels, chunk, total.shape[1])
            if old is not None:
                total = total + old[:, span, :]
            out_ref[:, span, :] = total
        else:
            for channel in range(channels):
                left = holds[index % 2][block, channel]
                total = jnp.dot(left, right, preferred_element_type=F32)
                if old is not None:
                    total = total + old[channel, span, :]
                out_ref[channel, span, :] = total

    def loop(body):
        def step(block, carry):
            body(block)
            return carry

        lax.fori_loop(0, blocks, step, 0)

    count = len(shifts)
    join(0)
    loop(functools.partial(fill, 0))
    for index in range(count):
        if index + 1 < count:
            join(index + 1)

            def both(block, index=index):
                multiply(index, block)
                fill(index + 1, block)

            loop(both)
        else:
            loop(functools.partial(multiply, index))


def reduce_kernel(own_ref, core_ref, far_ref, wide_ref, inv_ref, pick_ref, out_ref):
    grad = own_ref[...] + core_ref[...].astype(F32) + far_ref[...].astype(F32)
    wide = wide_ref[...]
    first = jnp.mean(grad, axis=1, keepdims=True)
    second = jnp.mean(grad * wide, axis=1, keepdims=True)
    row_grad = (inv_ref[:, 0:1] * (grad - first - wide * second)).astype(BF)
    own = row_grad.shape[0]
    back = jnp.dot(pick_ref[:, 0:own], row_grad, preferred_element_type=F32)
    out_ref[...] = back.astype(BF).reshape(out_ref.shape)


def place_kernel(at_ref, back_ref, out_ref):
    total = back_ref.shape[0] * back_ref.shape[1]
    count = at_ref.shape[1]
    pick = (lax.broadcasted_iota(jnp.int32, (total, count), 0) == at_ref[...]).astype(F32)
    back = back_ref[...].reshape(total, back_ref.shape[2])
    out_ref[...] = lax.dot_general(
        pick.astype(BF), back, (((0,), (0,)), ((), ())), preferred_element_type=F32
    ).astype(BF)


def ring_of(n_dp):
    if n_dp == 8:
        return [0, 2, 4, 6, 7, 5, 3, 1]
    order = []
    for block in range(n_dp // 4):
        line = list(range(block * 4, block * 4 + 4))
        order += line if block % 2 == 0 else line[::-1]
    return order


def on_device(patches, kept_mask, destination, coefficients, cotangent):
    n_dp = lax.axis_size("dp")
    n_mp = lax.axis_size("mp")
    img_dev, block_len, features = patches.shape
    channels, _, hidden = coefficients.shape
    capacity = img_dev * (KEEP_IMG // n_mp + KEEP_IMG // (2 * n_mp)) // n_dp
    slots = -(-(capacity + 1) // 8) * 8
    own = img_dev * (KEEP_IMG // n_mp)
    all_rows = own * n_mp
    patch_count = img_dev * block_len
    share = features // n_dp
    width = -(-own // 128) * 128

    ring = ring_of(n_dp)
    n_steps = n_dp // 2
    place = {device: index for index, device in enumerate(ring)}
    table = np.zeros((n_dp, n_mp, 4 + n_dp), np.int32)
    for device in range(n_dp):
        for part in range(n_mp):
            for k in range(4):
                table[device, part, k] = part ^ k
            for shift in range(n_dp):
                table[device, part, 4 + shift] = ring[(place[device] - shift) % n_dp]
    index = lax.axis_index("dp") * n_mp + lax.axis_index("mp")
    meta = lax.dynamic_index_in_dim(
        jnp.asarray(table.reshape(n_dp * n_mp, -1)), index, 0, keepdims=False
    )
    forth = [(ring[i], ring[(i + 1) % n_dp]) for i in range(n_dp)]
    back = [(b, a) for a, b in forth]
    swap_core = [(i, i ^ 1) for i in range(n_mp)]
    swap_far = [(i, i ^ 2) for i in range(n_mp)]

    def vm(shape, dtype):
        return jax.ShapeDtypeStruct(shape, dtype)

    outgoing, at = pl.pallas_call(
        functools.partial(send_kernel, n_dp, slots, capacity),
        out_shape=(vm((n_dp * slots, features), BF), vm((1, patch_count), jnp.int32)),
        compiler_params=PARAMS,
        cost_estimate=cost(2 * n_dp * slots * patch_count * features, 4 * 2**20),
        name="send",
    )(kept_mask, destination, patches.reshape(patch_count, features))
    arrived = lax.all_to_all(
        outgoing.reshape(n_dp, slots, features), "dp", split_axis=0, concat_axis=0
    )

    rounds = []
    right = left = cotangent
    for _ in range(n_steps - 1):
        right = lax.ppermute(right, "dp", forth)
        left = lax.ppermute(left, "dp", back)
        rounds.append((right, left))
    half = all_rows // 2
    rounds.append(
        (lax.ppermute(right[:half], "dp", forth), lax.ppermute(left[half:], "dp", back))
    )

    group = 3
    hidden_grads = []
    for first in range(0, channels, group):
        hidden_grads.append(
            pl.pallas_call(
                hidden_kernel,
                grid=(group,),
                in_specs=[
                    pl.BlockSpec((all_rows, hidden), lambda c: (0, 0)),
                    pl.BlockSpec((1, features, hidden), lambda c, first=first: (c + first, 0, 0)),
                ],
                out_specs=pl.BlockSpec((1, all_rows, features), lambda c: (c, 0, 0)),
                out_shape=vm((group, all_rows, features), BF),
                compiler_params=PARAMS,
                cost_estimate=cost(
                    2 * group * all_rows * features * hidden,
                    group * features * (hidden + all_rows) * 2,
                ),
                name="hidden",
            )(cotangent, coefficients)
        )

    arrived, meta, *hidden_grads = lax.optimization_barrier((arrived, meta, *hidden_grads))
    normed, feats, centred, inv_scale, pick = pl.pallas_call(
        functools.partial(arrive_kernel, n_dp, slots, capacity, own),
        out_shape=(
            vm((own, features), BF),
            vm((n_dp, share // 2, 2 * own), BF),
            vm((own, features), F32),
            vm((own, 128), F32),
            vm((n_dp * slots, width), BF),
        ),
        scratch_shapes=[pltpu.VMEM((n_dp * slots, width), F32)],
        compiler_params=PARAMS,
        cost_estimate=cost(2 * n_dp * slots * width * features, 4 * 2**20),
        name="arrive",
    )(arrived)

    norm_core = lax.ppermute(normed, "mp", swap_core)
    norm_far = lax.ppermute(normed, "mp", swap_far)
    norm_diag = lax.ppermute(norm_far, "mp", swap_core)

    def slope(values, k, dtype):
        block = 256
        return pl.pallas_call(
            functools.partial(slope_kernel, len(hidden_grads)),
            grid_spec=pltpu.PrefetchScalarGridSpec(
                num_scalar_prefetch=1,
                grid=(features // block,),
                in_specs=[
                    pl.BlockSpec((group, own, block), lambda f, meta, k=k: (0, meta[k], f))
                    for _ in hidden_grads
                ]
                + [pl.BlockSpec((own, block), lambda f, meta: (0, f))],
                out_specs=pl.BlockSpec((own, block), lambda f, meta: (0, f)),
            ),
            out_shape=vm((own, features), dtype),
            compiler_params=PARAMS,
            cost_estimate=cost(4e9, channels * own * features * 2),
            name="slope",
        )(meta, *hidden_grads, values)

    part_core = slope(norm_core, 1, BF)
    part_own = slope(normed, 0, F32)
    norm_diag, norm_far, part_core, part_own = lax.optimization_barrier(
        (norm_diag, norm_far, part_core, part_own)
    )
    part_diag = slope(norm_diag, 3, BF)
    part_far = slope(norm_far, 2, F32)
    got_own = lax.ppermute(part_core, "mp", swap_core)
    got_far = lax.ppermute(part_diag, "mp", swap_core)
    far_sum = (part_far + got_far.astype(F32)).astype(BF)
    got_sum = lax.ppermute(far_sum, "mp", swap_far)

    back_slots = pl.pallas_call(
        reduce_kernel,
        out_shape=vm((n_dp, slots, features), BF),
        compiler_params=PARAMS,
        cost_estimate=cost(2 * n_dp * slots * own * features, 4 * 2**20),
        name="reduce",
    )(part_own, got_own, got_sum, centred, inv_scale, pick)
    returned = lax.all_to_all(back_slots, "dp", split_axis=0, concat_axis=0)
    owner_rows = pl.pallas_call(
        place_kernel,
        out_shape=vm((patch_count, features), BF),
        compiler_params=PARAMS,
        cost_estimate=cost(2 * n_dp * slots * patch_count * features, 3 * 2**20),
        name="place",
    )(at, returned)

    feat_own = lax.all_to_all(feats, "dp", split_axis=0, concat_axis=0)
    feat_core = lax.ppermute(feat_own, "mp", swap_core)
    feat_far = lax.ppermute(feat_own, "mp", swap_far)
    feat_diag = lax.ppermute(feat_far, "mp", swap_core)
    values = (feat_own, feat_core, feat_far, feat_diag)
    chunk = 32 if share % 32 == 0 else share

    def table_sum(items, halves, running):
        whole = pl.BlockSpec((channels, share, hidden), lambda i, meta: (0, 0, 0))
        extra = [] if running is None else [running]
        cots = [cot for _, parts in items for cot in parts]
        value_spec = pl.BlockSpec((n_dp, share // 2, 2 * own), lambda i, meta: (0, 0, 0))
        hold = pltpu.VMEM((share // chunk, channels, chunk, all_rows), BF)
        return pl.pallas_call(
            functools.partial(
                table_kernel, [shift for shift, _ in items], halves, bool(extra), own, chunk
            ),
            grid_spec=pltpu.PrefetchScalarGridSpec(
                num_scalar_prefetch=1,
                grid=(1,),
                in_specs=[value_spec] * 4
                + [pl.BlockSpec(cot.shape, lambda i, meta: (0, 0)) for cot in cots]
                + [whole] * len(extra),
                out_specs=whole,
                scratch_shapes=[
                    hold,
                    hold,
                    pltpu.VMEM((share, all_rows), F32),
                    pltpu.VMEM((2, all_rows, hidden), BF),
                ],
            ),
            out_shape=vm((channels, share, hidden), F32),
            compiler_params=PARAMS,
            cost_estimate=cost(
                2 * channels * share * hidden * all_rows * len(items), 10 * 2**20
            ),
            name="table",
        )(meta, *values, *cots, *extra)

    running = None
    items = [(0, (cotangent,))]
    for step, (right, left) in enumerate(rounds, 1):
        if step < n_steps:
            items += [(step, (right,)), (n_dp - step, (left,))]
        else:
            items += [(step, (right, left))]
        if step % 2 == 0:
            running = table_sum(items, len(items) - 1 if step == n_steps else -1, running)
            items = []

    return (owner_rows.reshape(img_dev, block_len, features), running)


def solution(mesh):
    in_specs = (
        P("dp", "mp", None),
        P("dp", "mp"),
        P("dp", "mp"),
        P(None, None, "mp"),
        P("dp", "mp"),
    )
    out_specs = (P("dp", "mp", None), P(None, "dp", "mp"))
    return jax.shard_map(
        on_device, mesh=mesh, in_specs=in_specs, out_specs=out_specs, check_vma=False
    )
```
